512 devices in a mesh: dp: 64 (over y, z), mp: 8 (over x, core).
Axes of the slice: x: 4, y: 4, z: 16, core: 2. Of those that a mesh axis runs over, the one named last changes fastest.
Arguments:
- train_in: bfloat16 [4096, 64, 16], P('dp'), may hold values from -6 to 6
- train_out_grad: bfloat16 [4096, 64, 1024], P('dp', None, 'mp'), may hold values from -6 to 6
- query_in: bfloat16 [4096, 64, 16], P('dp'), may hold values from -6 to 6
- query_out_grad: bfloat16 [4096, 64, 1024], P('dp', None, 'mp'), may hold values from -6 to 6
- query_owner: int32 [4096, 1], P('dp'), may hold values from 0 to 63; in each aligned block of 64 rows (0 to 63, 64 to 127, ...) at most 2 rows name the same one
- sketch_seed: int32 [1], replicated, may hold values from 0 to 1073741823
Outputs:
- kernel: float32 [4096, 4096], P('mp', 'dp')
- owner_scores: float32 [64, 64, 2, 64], P('dp')
The draws below stay inside these ranges and needn't reach their ends.
Inputs may be any that keep to these rules, and one draw needn't show every extreme that they name: `query_owner`: within the queries of one device (aligned blocks of 64), one owner is named at most 2 times, a bound that some block reaches in every draw.
All inputs are finite; a program needn't handle non-finite values.
Results may differ from the reference program's by a relative error of at most 0.0041.
Values may be sent and summed in bfloat16 or wider, within the bound.
No kernel may reach another device: no remote copies, remote signals or barrier semaphores. Data moves between devices by JAX's collectives and lax.ppermute only.
A program may use at most 64 MiB of HBM per device.

```python
import math
import jax
import jax.numpy as jnp
import numpy as np
from jax import lax

VW = 1024
R = 16
K = 8192
L = 64
EX_DEV = 64
QX_DEV = 64
TRAIN_ROWS = 4096
QUERY_ROWS = 4096
CAP = 2
N_DP = 64


def block_levels(rng, extent, pieces, smallest, largest):
    def one(position, parts):
        draws = jax.random.uniform(jax.random.fold_in(jax.random.fold_in(rng, 6), position), (parts,), jnp.float32, smallest / len(pieces), largest / len(pieces))
        return jnp.repeat(jnp.exp(draws), extent[position] // parts).reshape((-1,) + (1,) * (len(extent) - position - 1))

    loudness = one(*pieces[0])
    for cut in pieces[1:]:
        loudness = loudness * one(*cut)
    return loudness


def routed_block(stream_key, own, number, rows, amount, top, limit, lean):
    ranking = jax.random.permutation(stream_key, amount)
    crowded, common = shares(amount, rows * top, limit, lean, True), shares(amount, rows * top, limit, lean, False)
    places = jnp.arange(amount)

    def named(sizes, turn):
        used = int((sizes > 0).sum())
        fixed = max(1, used // 4)
        shifted = fixed + (places - fixed + turn * (used - fixed)) % max(1, amount - fixed)
        return jnp.zeros((amount,), jnp.int32).at[ranking[jnp.where(places < fixed, places, shifted)]].set(jnp.asarray(sizes, jnp.int32))

    sizes = jnp.where(number % 4 == 0, named(crowded, number // 4), named(common, number - number // 4 - 1))
    mixed = jax.random.permutation(jax.random.fold_in(own, 3), amount)
    giver, taker = mixed[0:amount // 2 * 2:2], mixed[1:amount // 2 * 2:2]
    margin = jnp.minimum(sizes[giver] - 1, limit - sizes[taker]) // 2
    margin = jnp.where((giver == ranking[0]) | (taker == ranking[0]) | (sizes[taker] == 0), 0, jnp.maximum(margin, 0))
    shifted = jax.random.randint(jax.random.fold_in(own, 4), (amount // 2,), 0, 1 << 20) % (margin + 1)
    sizes = sizes.at[giver].add(-shifted).at[taker].add(shifted)
    items = jnp.searchsorted(jnp.cumsum(sizes), jnp.arange(rows * top), side="right").astype(jnp.int32)
    listing = items.reshape(top, rows).T
    listing = listing[jax.random.permutation(jax.random.fold_in(own, 1), rows)]
    turn = jax.random.randint(jax.random.fold_in(own, 2), (rows, 1), 0, top)
    return jnp.take_along_axis(listing, (jnp.arange(top)[None, :] + turn) % top, axis=1)


def shares(number_of, total, bound, lean, full):
    portions = [(1 << 20) // math.isqrt(grade ** lean) + 1 for grade in range(1, number_of + 1)]
    largest = bound if full else min(bound, max(-(-total // number_of), total * portions[0] // sum(portions)))
    least = 1 if total - largest >= number_of - 1 else 0
    holding, rest = [largest] + [least] * (number_of - 1), total - largest - least * (number_of - 1)
    while rest > 0:
        free = [i for i in range(1, number_of) if holding[i] < largest] or [i for i in range(1, number_of) if holding[i] < bound]
        mass, remaining = sum([portions[i] for i in free]), rest
        for i in free:
            extra = min(bound - holding[i], max(1, remaining * portions[i] // mass), rest)
            holding[i] = holding[i] + extra
            rest = rest - extra
    return np.array(holding)


def centred(rng, shape, spread, most, split=(), kind=jnp.bfloat16):
    loudness = block_levels(rng, shape, split, -0.22, 0.18) if split else 1.0
    array = jax.random.normal(rng, shape, jnp.float32) * spread * loudness
    return jnp.minimum(jnp.maximum(array, -most), most).astype(kind)


def setup_inputs(seed: int = 0) -> dict:
    keys = jax.random.split(jax.random.key(seed), 7)
    train_in = centred(keys[0], (TRAIN_ROWS, L, R), 1.0, 6.0, ((0, 64),))
    train_out_grad = centred(keys[1], (TRAIN_ROWS, L, VW), 1.0, 6.0, ((0, 64), (2, 8)))
    query_in = centred(keys[2], (QUERY_ROWS, L, R), 1.0, 6.0, ((0, 64),))
    query_out_grad = centred(keys[3], (QUERY_ROWS, L, VW), 1.0, 6.0, ((0, 64), (2, 8)))
    query_owner_keys = jax.random.split(jax.random.fold_in(keys[4], 1), QUERY_ROWS // QX_DEV)
    query_owner_turns = jax.random.permutation(jax.random.fold_in(keys[4], 3), QUERY_ROWS // QX_DEV)
    query_owner = jax.vmap(lambda own, number: routed_block(jax.random.fold_in(keys[4], 2), own, number, QX_DEV, N_DP, 1, CAP, 2))(query_owner_keys, query_owner_turns).reshape((QUERY_ROWS, 1))
    sketch_seed = jax.random.randint(keys[5], (1,), 0, 1073741824).astype(jnp.int32)
    return {"train_in": train_in, "train_out_grad": train_out_grad, "query_in": query_in, "query_out_grad": query_out_grad, "query_owner": query_owner, "sketch_seed": sketch_seed}


hash_factor = 73244475

def sign_table(coords, columns, seed_word):
    mixing = coords[:, None] * K + columns[None, :] ^ seed_word
    for round_index in range(2):
        mixing = mixing * hash_factor
        mixing = mixing ^ lax.shift_right_logical(mixing, jnp.full_like(mixing, 16))
    return (1 - 2 * (mixing & 1)).astype(jnp.bfloat16)

def local_grads(packed):
    inputs, out_grads = packed
    return jnp.einsum('ntr,ntj->nrj', inputs.astype(jnp.float32), out_grads.astype(jnp.float32)).astype(jnp.bfloat16)

def reference(train_in, train_out_grad, query_in, query_out_grad, query_owner, sketch_seed):
    seed_word = sketch_seed[0]
    train_grads = lax.map(local_grads, (train_in.reshape(N_DP, EX_DEV, L, R), train_out_grad.reshape(N_DP, EX_DEV, L, VW)))
    train_grads = train_grads.reshape(TRAIN_ROWS, R * VW)
    query_grads = lax.map(local_grads, (query_in.reshape(N_DP, QX_DEV, L, R), query_out_grad.reshape(N_DP, QX_DEV, L, VW)))
    query_grads = query_grads.reshape(N_DP, QX_DEV, R * VW)
    coords = lax.iota(jnp.int32, R * VW)
    step_cols = min(1024, K)

    def project_block(offset):
        columns = offset + lax.iota(jnp.int32, step_cols)
        return jnp.dot(train_grads, sign_table(coords, columns, seed_word), preferred_element_type=jnp.float32)
    col_blocks = lax.map(project_block, jnp.arange(0, K, step_cols, dtype=jnp.int32))
    feature_scale = 1.0 / math.sqrt(L * R * VW)
    features = (jnp.transpose(col_blocks, (1, 0, 2)).reshape(TRAIN_ROWS, K) * feature_scale).astype(jnp.bfloat16)
    kernel = jnp.dot(features, features.T, preferred_element_type=jnp.float32) * (1.0 / math.sqrt(K))
    owners = query_owner[:, 0].reshape(N_DP, QX_DEV)
    later_index = lax.broadcasted_iota(jnp.int32, (QX_DEV, QX_DEV), 0)
    earlier = lax.broadcasted_iota(jnp.int32, (QX_DEV, QX_DEV), 1) < later_index
    same_owner = owners[:, :, None] == owners[:, None, :]
    slot_rank = lax.optimization_barrier(jnp.sum((same_owner & earlier[None]).astype(jnp.int32), axis=2))
    train_by_owner = train_grads.reshape(N_DP, EX_DEV, R * VW)

    def score_device(packed):
        grads_here, owners_here = packed
        chosen = train_by_owner[owners_here]
        return jnp.einsum('qc,qnc->qn', grads_here.astype(jnp.float32), chosen.astype(jnp.float32), precision=lax.Precision.HIGHEST)
    scores = lax.map(score_device, (query_grads, owners))
    score_scale = 1.0 / (L * math.sqrt(R * VW))
    sources = lax.broadcasted_iota(jnp.int32, (N_DP, QX_DEV), 0)
    owner_scores = jnp.zeros((N_DP, N_DP, CAP, EX_DEV), jnp.float32)
    owner_scores = owner_scores.at[owners, sources, slot_rank].set(scores * score_scale)
    return (kernel, owner_scores)
```

```python
import math

import jax
import jax.numpy as jnp
from jax import lax
from jax.sharding import Mesh
from jax.sharding import PartitionSpec as P

VW = 1024
R = 16
K = 8192
L = 64
DP = ("y", "zh", "zl")
MP = ("x", "c")
Z = ("zh", "zl")

hash_factor = 73244475
sign_factor = ((hash_factor + (1 << 16)) << 15) % (1 << 32)
sign_factor = sign_factor - (1 << 32) if sign_factor >= (1 << 31) else sign_factor


def swap(parts, axes):
    return lax.all_to_all(parts, axes, split_axis=0, concat_axis=0, tiled=True)


def from_everyone(value, axes):
    return swap(jnp.broadcast_to(value, (lax.axis_size(axes), *value.shape)), axes)


def sign_table(coords, columns, seed_word):
    high = ((coords ^ lax.shift_right_logical(seed_word, 13)) << 13) * hash_factor
    low = (columns ^ (seed_word & (K - 1))) * hash_factor
    mixed = high[:, None] + low[None, :]
    mixed = mixed ^ lax.shift_right_logical(mixed, jnp.full_like(mixed, 16))
    mixed = mixed * sign_factor
    return jnp.where(mixed < 0, -1.0, 1.0).astype(jnp.bfloat16)


def local_grads(inputs, out_grads):
    return jnp.einsum("ntr,ntj->nrj", inputs, out_grads, preferred_element_type=jnp.float32).astype(
        jnp.bfloat16
    )


def shards(train_in, train_out_grad, query_in, query_out_grad, query_owner, sketch_seed):
    examples, _, width = train_out_grad.shape
    queries = query_in.shape[0]
    ny, nzh, nzl, nx, nc = (lax.axis_size(a) for a in ("y", "zh", "zl", "x", "c"))
    nz = nzh * nzl
    coords_here = R * width

    train_grads = local_grads(train_in, train_out_grad)
    by_y = from_everyone(train_grads, "y")

    query_grads = local_grads(query_in, query_out_grad)
    owners = query_owner[:, 0]
    later = lax.broadcasted_iota(jnp.int32, (queries, queries), 0)
    earlier = (owners[:, None] == owners[None, :]) & (
        lax.broadcasted_iota(jnp.int32, (queries, queries), 1) < later
    )
    slot = jnp.sum(earlier.astype(jnp.int32), axis=1)
    capacity = 2
    target = ((owners % nz) * ny + owners // nz) * capacity + slot
    placing = (
        lax.broadcasted_iota(jnp.int32, (ny * nz * capacity, queries), 0) == target[None, :]
    ).astype(jnp.bfloat16)
    outgoing = jnp.dot(
        placing, query_grads.reshape(queries, coords_here), preferred_element_type=jnp.float32
    ).astype(jnp.bfloat16)
    arrived = swap(outgoing.reshape(nz, ny * capacity, coords_here), Z)
    arrived = arrived.reshape(nz, ny, capacity, coords_here).swapaxes(0, 1)

    seed_word = sketch_seed[0]
    block_cols = K // ny
    columns = lax.axis_index("y") * block_cols + lax.iota(jnp.int32, block_cols)
    first = lax.axis_index(MP) * width
    coords = (
        lax.broadcasted_iota(jnp.int32, (R, width), 0) * VW
        + lax.broadcasted_iota(jnp.int32, (R, width), 1)
        + first
    ).reshape(-1)
    signs = lax.optimization_barrier(sign_table(coords, columns, seed_word))
    partial = jnp.dot(
        by_y.reshape(ny * examples, coords_here), signs, preferred_element_type=jnp.float32
    )
    partial = partial.astype(jnp.bfloat16).reshape(ny, examples, nc, block_cols // nc)
    partial = partial.transpose(0, 2, 1, 3).reshape(ny * nc, examples, block_cols // nc)
    feature_scale = 1.0 / math.sqrt(L * R * VW)
    features = (swap(partial, MP).astype(jnp.float32).sum(axis=0) * feature_scale).astype(
        jnp.bfloat16
    )

    near = from_everyone(features, "zl")
    rows = from_everyone(features, "zh")
    cols = from_everyone(near, "x")
    depth = features.shape[1]
    gram = jnp.einsum(
        "ymk,ank->yamn",
        cols.reshape(nx, nzl * examples, depth),
        rows.reshape(nc, (nzh // nc) * examples, depth),
        preferred_element_type=jnp.float32,
    )
    gram = swap(gram.reshape(ny * nc, nzl * examples, -1), ("y", "c")).sum(axis=0)
    gram = swap(gram.reshape(nzl, examples, -1), "zl") * (1.0 / math.sqrt(K))
    gram = gram.reshape(nzl, examples, nzh // nc, examples).transpose(2, 0, 3, 1)
    gram = gram.reshape(-1, examples)

    arrived = swap(arrived.reshape(ny, nz * capacity, coords_here), "y")
    scores = jnp.einsum(
        "ic,nc->in",
        arrived.reshape(ny * nz * capacity, coords_here),
        train_grads.reshape(examples, coords_here),
        preferred_element_type=jnp.float32,
    )
    score_scale = 1.0 / (L * math.sqrt(R * VW))
    scores = from_everyone(scores.reshape(-1, 2 * examples), MP).sum(axis=0) * score_scale
    return gram, scores.reshape(1, ny * nz, capacity, examples)


def solution(mesh):
    finer = Mesh(mesh.devices.reshape(4, 4, 4, 4, 2), ("y", "zh", "zl", "x", "c"))
    placed = (
        P(DP, None, None),
        P(DP, None, MP),
        P(DP, None, None),
        P(DP, None, MP),
        P(DP, None),
        P(),
    )
    return jax.shard_map(
        shards,
        mesh=finer,
        in_specs=placed,
        out_specs=(P(MP, DP), P(DP, None, None, None)),
        check_vma=False,
    )
```

```python
import math

import jax
import jax.numpy as jnp
from jax import lax
from jax.sharding import Mesh
from jax.sharding import PartitionSpec as P


VW = 1024
R = 16
K = 8192
L = 64
DP = ("y", "zh", "zl")
MP = ("x", "c")
Z = ("zh", "zl")

hash_factor = 73244475
sign_factor = ((hash_factor + (1 << 16)) << 15) % (1 << 32)
sign_factor = sign_factor - (1 << 32) if sign_factor >= (1 << 31) else sign_factor


def swap(parts, axes):
    return lax.all_to_all(parts, axes, split_axis=0, concat_axis=0, tiled=True)


def from_everyone(value, axes):
    return swap(jnp.broadcast_to(value, (lax.axis_size(axes), *value.shape)), axes)


def shifted(value, axes, shift):
    size = lax.axis_size(axes)
    return lax.ppermute(value, axes, [(k, (k + shift) % size) for k in range(size)])


def placed_at(parts, places):
    out = jnp.zeros((len(parts), *parts[0].shape), parts[0].dtype)
    for part, place in zip(parts, places, strict=True):
        out = lax.dynamic_update_slice_in_dim(out, part[None], place, 0)
    return out


def part_of(parts, place):
    return lax.dynamic_index_in_dim(parts, place, 0, keepdims=False)


def sign_table(coords, columns, seed_word):
    high = ((coords ^ lax.shift_right_logical(seed_word, 13)) << 13) * hash_factor
    low = (columns ^ (seed_word & (K - 1))) * hash_factor
    mixed = high[:, None] + low[None, :]
    mixed = mixed ^ lax.shift_right_logical(mixed, jnp.full_like(mixed, 16))
    mixed = mixed * sign_factor
    return jnp.where(mixed < 0, -1.0, 1.0).astype(jnp.bfloat16)


def local_grads(inputs, out_grads):
    return jnp.einsum("ntr,ntj->nrj", inputs, out_grads, preferred_element_type=jnp.float32).astype(
        jnp.bfloat16
    )


def shards(train_in, train_out_grad, query_in, query_out_grad, query_owner, sketch_seed):
    examples, _, width = train_out_grad.shape
    queries = query_in.shape[0]
    ny, nzh, nzl, nx, nc = (lax.axis_size(a) for a in ("y", "zh", "zl", "x", "c"))
    nz = nzh * nzl
    coords_here = R * width

    train_grads = local_grads(train_in, train_out_grad)
    x, y, c, zh, _ = (lax.axis_index(a) for a in ("x", "y", "c", "zh", "zl"))
    by_y = [train_grads] + [shifted(train_grads, "y", -k) for k in range(1, ny)]
    by_y = jnp.stack(by_y).reshape(ny * examples, coords_here)

    query_grads = local_grads(query_in, query_out_grad)
    owners = query_owner[:, 0]
    later = lax.broadcasted_iota(jnp.int32, (queries, queries), 0)
    earlier = (owners[:, None] == owners[None, :]) & (
        lax.broadcasted_iota(jnp.int32, (queries, queries), 1) < later
    )
    slot = jnp.sum(earlier.astype(jnp.int32), axis=1)
    capacity = 2
    target = ((owners % nz) * ny + owners // nz) * capacity + slot
    placing = (
        lax.broadcasted_iota(jnp.int32, (ny * nz * capacity, queries), 0) == target[None, :]
    ).astype(jnp.bfloat16)
    outgoing = jnp.dot(
        placing, query_grads.reshape(queries, coords_here), preferred_element_type=jnp.float32
    ).astype(jnp.bfloat16)
    arrived = swap(outgoing.reshape(nz, ny * capacity, coords_here), Z)
    arrived = arrived.reshape(nz, ny, capacity, coords_here).swapaxes(0, 1)

    seed_word = sketch_seed[0]
    half_cols = K // ny // nc
    first = lax.axis_index(MP) * width
    coords = (
        lax.broadcasted_iota(jnp.int32, (R, width), 0) * VW
        + lax.broadcasted_iota(jnp.int32, (R, width), 1)
        + first
    ).reshape(-1)
    halves = []
    for half in (1 - c, c):
        columns = (y * nc + half) * half_cols + lax.iota(jnp.int32, half_cols)
        signs = sign_table(coords, columns, seed_word)
        signs = lax.optimization_barrier(signs)
        halves.append(jnp.dot(by_y, signs, preferred_element_type=jnp.float32))
    traded = shifted(halves[0].astype(jnp.bfloat16), "c", 1)
    partial = lax.optimization_barrier(halves[1]) + traded.astype(jnp.float32)
    partial = partial.reshape(ny, examples, half_cols)
    turn = x - y + ny
    features = part_of(partial, lax.rem(turn, ny))
    sent = [
        shifted(part_of(partial, lax.rem(turn + k, ny)).astype(jnp.bfloat16), "x", k)
        for k in range(1, nx)
    ]
    for part in sent:
        features = features + part.astype(jnp.float32)
    feature_scale = 1.0 / math.sqrt(L * R * VW)
    features = (features * feature_scale).astype(jnp.bfloat16)

    near = from_everyone(features, "zl").reshape(nzl * examples, -1)
    above, below = shifted(features, Z, -nzl), shifted(features, Z, nzl)
    cols = jnp.stack([near] + [shifted(near, "x", -k) for k in range(1, nx)])
    cut = examples // 2
    opposite = [shifted(above[:cut], Z, -nzl), shifted(below[cut:], Z, nzl)]
    opposite = jnp.concatenate(opposite, axis=0)
    rows = placed_at(
        [features, above, opposite, below], [lax.rem(zh + k, nzh) ^ (c * 2) for k in range(nzh)]
    )
    rows = rows.reshape(nc, (nzh // nc) * examples, -1)
    kept, given = (
        jnp.einsum("tmk,nk->tmn", cols, rows[h], preferred_element_type=jnp.float32)
        for h in range(nc)
    )
    traded = shifted(given.astype(jnp.bfloat16), "c", 1)
    gram = lax.optimization_barrier(kept) + traded.astype(jnp.float32)
    gram = jnp.stack([part_of(gram, lax.rem(k - x + nx, nx)) for k in range(ny)])
    gram = gram.astype(jnp.bfloat16).reshape(ny * nzl, examples, -1)
    gram = swap(gram, ("y", "zl"))
    gram = gram.reshape(ny, nzl, examples, -1).astype(jnp.float32).sum(axis=0)
    gram = gram * (1.0 / math.sqrt(K))
    gram = gram.reshape(nzl, examples, nzh // nc, examples).transpose(2, 0, 3, 1)
    gram = gram.reshape(-1, examples)

    arrived = swap(arrived.reshape(ny, nz * capacity, coords_here), "y")
    scores = jnp.einsum(
        "ic,nc->in",
        arrived.reshape(ny * nz * capacity, coords_here),
        train_grads.reshape(examples, coords_here),
        preferred_element_type=jnp.float32,
    )
    score_scale = 1.0 / (L * math.sqrt(R * VW))
    scores = from_everyone(scores.reshape(-1, 2 * examples), MP)
    scores = scores.sum(axis=0) * score_scale
    return gram, scores.reshape(1, ny * nz, capacity, examples)


def solution(mesh):
    finer = Mesh(mesh.devices.reshape(4, 4, 4, 4, 2), ("y", "zh", "zl", "x", "c"))
    placed = (
        P(DP, None, None),
        P(DP, None, MP),
        P(DP, None, None),
        P(DP, None, MP),
        P(DP, None),
        P(),
    )
    return jax.shard_map(
        shards,
        mesh=finer,
        in_specs=placed,
        out_specs=(P(MP, DP), P(DP, None, None, None)),
        check_vma=False,
    )
```

```python
import math

import jax
import jax.numpy as jnp
from jax import lax
from jax.experimental import pallas as pl
from jax.experimental.pallas import tpu as pltpu
from jax.sharding import Mesh
from jax.sharding import PartitionSpec as P


VW = 1024
R = 16
K = 8192
L = 64
DP = ("y", "zh", "zl")
MP = ("x", "c")

hash_factor = 73244475
sign_factor = ((hash_factor + (1 << 16)) << 15) % (1 << 32)
sign_factor = sign_factor - (1 << 32) if sign_factor >= (1 << 31) else sign_factor


def swap(parts, axes):
    return lax.all_to_all(parts, axes, split_axis=0, concat_axis=0, tiled=True)


def from_everyone(value, axes):
    return swap(jnp.broadcast_to(value, (lax.axis_size(axes), *value.shape)), axes)


def shifted(value, axes, shift):
    size = lax.axis_size(axes)
    return lax.ppermute(value, axes, [(k, (k + shift) % size) for k in range(size)])


def placed_at(parts, places):
    out = jnp.zeros((len(parts), *parts[0].shape), parts[0].dtype)
    for part, place in zip(parts, places, strict=True):
        out = lax.dynamic_update_slice_in_dim(out, part[None], place, 0)
    return out


def part_of(parts, place):
    return lax.dynamic_index_in_dim(parts, place, 0, keepdims=False)


def sketch_kernel(where, *refs):
    pieces, out, total = refs[:-2], refs[-2], refs[-1]
    seed, first, start = where[0], where[1], where[2]
    depth, width = 2, pieces[0].shape[2]
    cols = out.shape[1]
    shape = (depth * width, 128)
    row = lax.broadcasted_iota(jnp.int32, shape, 0)
    coord = (row // width) * VW + row % width + first
    column = lax.broadcasted_iota(jnp.int32, (1, cols), 1) + start
    low = (column ^ (seed & (K - 1))) * hash_factor
    seed_high = lax.shift_right_logical(seed, 13)

    total[...] = jnp.zeros_like(total)

    def step(k, carry):
        high = (((coord + k * (depth * VW)) ^ seed_high) << 13) * hash_factor
        grads = jnp.concatenate(
            [jnp.concatenate([p[k * depth + d] for p in pieces], axis=0) for d in range(depth)],
            axis=1,
        )
        for t in range(0, cols, 256):
            tiles = []
            for u in range(t, t + 256, 128):
                mixed = high + low[:, u : u + 128]
                mixed = mixed ^ lax.shift_right_logical(mixed, 16)
                mixed = mixed * sign_factor
                tiles.append(jnp.where(mixed < 0, -1.0, 1.0).astype(jnp.bfloat16))
            signs = jnp.concatenate(tiles, axis=1)
            total[:, t : t + 256] += jnp.dot(grads, signs, preferred_element_type=jnp.float32)
        return carry

    lax.fori_loop(0, R // depth, step, 0)
    out[...] = total[...].astype(out.dtype)


def sketched(where, pieces, cols, dtype):
    rows = sum(p.shape[1] for p in pieces)
    flops = 2 * rows * cols * pieces[0].shape[0] * pieces[0].shape[2]
    return pl.pallas_call(
        sketch_kernel,
        out_shape=jax.ShapeDtypeStruct((rows, cols), dtype),
        in_specs=[pl.BlockSpec(memory_space=pltpu.SMEM)]
        + [pl.BlockSpec(memory_space=pltpu.VMEM)] * len(pieces),
        out_specs=pl.BlockSpec(memory_space=pltpu.VMEM),
        scratch_shapes=[pltpu.VMEM((rows, cols), jnp.float32)],
        cost_estimate=pl.CostEstimate(
            flops=flops, bytes_accessed=rows * cols * 4, transcendentals=0
        ),
        compiler_params=pltpu.CompilerParams(vmem_limit_bytes=24 << 20),
        name="sketch",
    )(where, *pieces)


def local_grads(inputs, out_grads):
    return jnp.einsum("ntr,ntj->nrj", inputs, out_grads, preferred_element_type=jnp.float32).astype(
        jnp.bfloat16
    )


def shards(train_in, train_out_grad, query_in, query_out_grad, query_owner, sketch_seed):
    examples, _, width = train_out_grad.shape
    queries = query_in.shape[0]
    ny, nzh, nzl, nx, nc = (lax.axis_size(a) for a in ("y", "zh", "zl", "x", "c"))
    nz = nzh * nzl
    coords_here = R * width

    train_grads = local_grads(train_in, train_out_grad)
    x, y, c, _, zl = (lax.axis_index(a) for a in ("x", "y", "c", "zh", "zl"))
    by_rank = train_grads.swapaxes(0, 1)
    pieces = [by_rank] + [shifted(by_rank, "y", -k) for k in range(1, ny)]

    query_grads = local_grads(query_in, query_out_grad)
    owners = query_owner[:, 0]
    later = lax.broadcasted_iota(jnp.int32, (queries, queries), 0)
    earlier = (owners[:, None] == owners[None, :]) & (
        lax.broadcasted_iota(jnp.int32, (queries, queries), 1) < later
    )
    slot = jnp.sum(earlier.astype(jnp.int32), axis=1)
    capacity = 2
    target = owners * capacity + slot
    placing = (
        lax.broadcasted_iota(jnp.int32, (ny * nz * capacity, queries), 0) == target[None, :]
    ).astype(jnp.bfloat16)
    outgoing = jnp.dot(
        placing, query_grads.reshape(queries, coords_here), preferred_element_type=jnp.float32
    ).astype(jnp.bfloat16)
    arrived = swap(outgoing.reshape(ny * nz, capacity, coords_here), DP)

    half_cols = K // ny // nc
    first = lax.axis_index(MP) * width
    halves = []
    for half, dtype in ((1 - c, jnp.bfloat16), (c, jnp.float32)):
        start = (y * nc + half) * half_cols
        where = jnp.stack([sketch_seed[0], first, start])
        halves.append(sketched(where, pieces, half_cols, dtype))
    traded = shifted(halves[0], "c", 1)
    partial = halves[1] + traded.astype(jnp.float32)
    partial = partial.reshape(ny, examples, half_cols)
    turn = x - y + ny
    features = part_of(partial, lax.rem(turn, ny))
    sent = [
        shifted(part_of(partial, lax.rem(turn + k, ny)).astype(jnp.bfloat16), "x", k)
        for k in range(1, nx)
    ]
    for part in sent:
        features = features + part.astype(jnp.float32)
    feature_scale = 1.0 / math.sqrt(L * R * VW)
    features = (features * feature_scale).astype(jnp.bfloat16)

    near = [features] + [shifted(features, "zl", -k) for k in range(1, nzl)]
    near = placed_at(near, [lax.rem(zl + k, nzl) for k in range(nzl)])
    near = near.reshape(nzl * examples, -1)
    rows = from_everyone(features, "zh").reshape(nc, (nzh // nc) * examples, -1)
    cols = jnp.stack([near] + [shifted(near, "x", -k) for k in range(1, nx)])
    kept, given = (
        jnp.einsum("tmk,nk->tmn", cols, part_of(rows, h), preferred_element_type=jnp.float32)
        for h in (c, 1 - c)
    )
    traded = shifted(given.astype(jnp.bfloat16), "c", 1)
    gram = lax.optimization_barrier(kept) + traded.astype(jnp.float32)
    gram = jnp.stack([part_of(gram, lax.rem(k - x + nx, nx)) for k in range(ny)])
    gram = gram.astype(jnp.bfloat16).reshape(ny * nzl, examples, -1)
    gram = swap(gram, ("y", "zl"))
    gram = gram.reshape(ny, nzl, examples, -1).astype(jnp.float32).sum(axis=0)
    gram = gram * (1.0 / math.sqrt(K))
    gram = gram.reshape(nzl, examples, nzh // nc, examples).transpose(2, 0, 3, 1)
    gram = gram.reshape(-1, examples)

    scores = jnp.einsum(
        "ic,nc->in",
        arrived.reshape(ny * nz * capacity, coords_here),
        train_grads.reshape(examples, coords_here),
        preferred_element_type=jnp.float32,
    )
    score_scale = 1.0 / (L * math.sqrt(R * VW))
    scores = scores.reshape(-1, 2 * examples)
    for axis, size, bit in (("c", nc, 1), ("x", nx, 1), ("x", nx, 2)):
        scores = scores + lax.ppermute(scores, axis, [(k, k ^ bit) for k in range(size)])
    scores = scores * score_scale
    return gram, scores.reshape(1, ny * nz, capacity, examples)


def solution(mesh):
    finer = Mesh(mesh.devices.reshape(4, 4, 4, 4, 2), ("y", "zh", "zl", "x", "c"))
    placed = (
        P(DP, None, None),
        P(DP, None, MP),
        P(DP, None, None),
        P(DP, None, MP),
        P(DP, None),
        P(),
    )
    return jax.shard_map(
        shards,
        mesh=finer,
        in_specs=placed,
        out_specs=(P(MP, DP), P(DP, None, None, None)),
        check_vma=False,
    )
```

```python
import math

import jax
import jax.numpy as jnp
from jax import lax
from jax.experimental import pallas as pl
from jax.experimental.pallas import tpu as pltpu
from jax.sharding import Mesh
from jax.sharding import PartitionSpec as P


VW = 1024
R = 16
K = 8192
L = 64
DP = ("y", "zh", "zl")
MP = ("x", "c")

hash_factor = 73244475
sign_factor = ((hash_factor + (1 << 16)) << 15) % (1 << 32)
sign_factor = sign_factor - (1 << 32) if sign_factor >= (1 << 31) else sign_factor


def swap(parts, axes):
    return lax.all_to_all(parts, axes, split_axis=0, concat_axis=0, tiled=True)


def from_everyone(value, axes):
    return swap(jnp.broadcast_to(value, (lax.axis_size(axes), *value.shape)), axes)


def shifted(value, axes, shift):
    size = lax.axis_size(axes)
    return lax.ppermute(value, axes, [(k, (k + shift) % size) for k in range(size)])


def placed_at(parts, places):
    out = jnp.zeros((len(parts), *parts[0].shape), parts[0].dtype)
    for part, place in zip(parts, places, strict=True):
        out = lax.dynamic_update_slice_in_dim(out, part[None], place, 0)
    return out


def part_of(parts, place):
    return lax.dynamic_index_in_dim(parts, place, 0, keepdims=False)


def sketch_kernel(where, *refs):
    pieces, out, total = refs[:-2], refs[-2], refs[-1]
    seed, first, start = where[0], where[1], where[2]
    depth, width = 2, pieces[0].shape[2]
    cols = out.shape[1]
    shape = (depth * width, 128)
    row = lax.broadcasted_iota(jnp.int32, shape, 0)
    coord = (row // width) * VW + row % width + first
    column = lax.broadcasted_iota(jnp.int32, (1, cols), 1) + start
    low = (column ^ (seed & (K - 1))) * hash_factor
    seed_high = lax.shift_right_logical(seed, 13)

    total[...] = jnp.zeros_like(total)

    def step(k, carry):
        high = (((coord + k * (depth * VW)) ^ seed_high) << 13) * hash_factor
        grads = jnp.concatenate(
            [jnp.concatenate([p[k * depth + d] for p in pieces], axis=0) for d in range(depth)],
            axis=1,
        )
        for t in range(0, cols, 256):
            tiles = []
            for u in range(t, t + 256, 128):
                mixed = high + low[:, u : u + 128]
                mixed = mixed ^ lax.shift_right_logical(mixed, 16)
                mixed = mixed * sign_factor
                tiles.append(jnp.where(mixed < 0, -1.0, 1.0).astype(jnp.bfloat16))
            signs = jnp.concatenate(tiles, axis=1)
            total[:, t : t + 256] += jnp.dot(grads, signs, preferred_element_type=jnp.float32)
        return carry

    lax.fori_loop(0, R // depth, step, 0, unroll=True)
    out[...] = total[...].astype(out.dtype)


def sketched(where, pieces, cols, dtype):
    rows = sum(p.shape[1] for p in pieces)
    flops = 2 * rows * cols * pieces[0].shape[0] * pieces[0].shape[2]
    return pl.pallas_call(
        sketch_kernel,
        out_shape=jax.ShapeDtypeStruct((rows, cols), dtype),
        in_specs=[pl.BlockSpec(memory_space=pltpu.SMEM)]
        + [pl.BlockSpec(memory_space=pltpu.VMEM)] * len(pieces),
        out_specs=pl.BlockSpec(memory_space=pltpu.VMEM),
        scratch_shapes=[pltpu.VMEM((rows, cols), jnp.float32)],
        cost_estimate=pl.CostEstimate(
            flops=flops, bytes_accessed=rows * cols * 4, transcendentals=0
        ),
        compiler_params=pltpu.CompilerParams(vmem_limit_bytes=24 << 20),
        name="sketch",
    )(where, *pieces)


def local_grads(inputs, out_grads):
    return jnp.einsum("ntr,ntj->nrj", inputs, out_grads, preferred_element_type=jnp.float32).astype(
        jnp.bfloat16
    )


def shards(train_in, train_out_grad, query_in, query_out_grad, query_owner, sketch_seed):
    examples, _, width = train_out_grad.shape
    queries = query_in.shape[0]
    ny, nzh, nzl, nx, nc = (lax.axis_size(a) for a in ("y", "zh", "zl", "x", "c"))
    nz = nzh * nzl
    coords_here = R * width

    train_grads = local_grads(train_in, train_out_grad)
    x, y, c, _, zl = (lax.axis_index(a) for a in ("x", "y", "c", "zh", "zl"))
    by_rank = train_grads.swapaxes(0, 1)
    pieces = [by_rank] + [shifted(by_rank, "y", -k) for k in range(1, ny)]

    query_grads = local_grads(query_in, query_out_grad)
    owners = query_owner[:, 0]
    later = lax.broadcasted_iota(jnp.int32, (queries, queries), 0)
    earlier = (owners[:, None] == owners[None, :]) & (
        lax.broadcasted_iota(jnp.int32, (queries, queries), 1) < later
    )
    slot = jnp.sum(earlier.astype(jnp.int32), axis=1)
    capacity = 2
    target = owners * capacity + slot
    placing = (
        lax.broadcasted_iota(jnp.int32, (ny * nz * capacity, queries), 0) == target[None, :]
    ).astype(jnp.bfloat16)
    outgoing = jnp.dot(
        placing, query_grads.reshape(queries, coords_here), preferred_element_type=jnp.float32
    ).astype(jnp.bfloat16)
    arrived = swap(outgoing.reshape(ny * nz, capacity, coords_here), DP)

    half_cols = K // ny // nc
    first = lax.axis_index(MP) * width
    halves = []
    for half, dtype in ((1 - c, jnp.bfloat16), (c, jnp.float32)):
        start = (y * nc + half) * half_cols
        where = jnp.stack([sketch_seed[0], first, start])
        halves.append(sketched(where, pieces, half_cols, dtype))
    traded = shifted(halves[0], "c", 1)
    kept, traded = (h.reshape(ny, examples, half_cols) for h in (halves[1], traded))
    turn = x - y + ny
    sums = [
        part_of(kept, lax.rem(turn + k, ny)) + part_of(traded, lax.rem(turn + k, ny)).astype(jnp.float32)
        for k in range(nx)
    ]
    features = sums[0]
    sent = [shifted(sums[k].astype(jnp.bfloat16), "x", k) for k in range(1, nx)]
    for part in sent:
        features = features + part.astype(jnp.float32)
    feature_scale = 1.0 / math.sqrt(L * R * VW)
    features = (features * feature_scale).astype(jnp.bfloat16)

    near = [features] + [shifted(features, "zl", -k) for k in range(1, nzl)]
    near = placed_at(near, [lax.rem(zl + k, nzl) for k in range(nzl)])
    near = near.reshape(nzl * examples, -1)
    rows = from_everyone(features, "zh").reshape(nc, (nzh // nc) * examples, -1)
    cols = jnp.stack([near] + [shifted(near, "x", -k) for k in range(1, nx)])
    kept, given = (
        jnp.einsum("tmk,nk->tmn", cols, part_of(rows, h), preferred_element_type=jnp.float32)
        for h in (c, 1 - c)
    )
    traded = shifted(given.astype(jnp.bfloat16), "c", 1)
    gram = lax.optimization_barrier(kept) + traded.astype(jnp.float32)
    gram = jnp.stack([part_of(gram, lax.rem(k - x + nx, nx)) for k in range(ny)])
    gram = gram.astype(jnp.bfloat16).reshape(ny * nzl, examples, -1)
    gram = swap(gram, ("y", "zl"))
    gram = gram.reshape(ny, nzl, examples, -1).astype(jnp.float32).sum(axis=0)
    gram = gram * (1.0 / math.sqrt(K))
    gram = gram.reshape(nzl, examples, nzh // nc, examples).transpose(2, 0, 3, 1)
    gram = gram.reshape(-1, examples)

    scores = jnp.einsum(
        "ic,nc->in",
        arrived.reshape(ny * nz * capacity, coords_here),
        train_grads.reshape(examples, coords_here),
        preferred_element_type=jnp.float32,
    )
    score_scale = 1.0 / (L * math.sqrt(R * VW))
    scores = scores.reshape(-1, 2 * examples)
    for axis, size, bit in (("c", nc, 1), ("x", nx, 1), ("x", nx, 2)):
        scores = scores + lax.ppermute(scores, axis, [(k, k ^ bit) for k in range(size)])
    scores = scores * score_scale
    return gram, scores.reshape(1, ny * nz, capacity, examples)


def solution(mesh):
    finer = Mesh(mesh.devices.reshape(4, 4, 4, 4, 2), ("y", "zh", "zl", "x", "c"))
    placed = (
        P(DP, None, None),
        P(DP, None, MP),
        P(DP, None, None),
        P(DP, None, MP),
        P(DP, None),
        P(),
    )
    return jax.shard_map(
        shards,
        mesh=finer,
        in_specs=placed,
        out_specs=(P(MP, DP), P(DP, None, None, None)),
        check_vma=False,
    )
```

```python
import math

import jax
import jax.numpy as jnp
from jax import lax
from jax.experimental import pallas as pl
from jax.experimental.pallas import tpu as pltpu
from jax.sharding import Mesh
from jax.sharding import PartitionSpec as P


VW = 1024
R = 16
K = 8192
L = 64
DP = ("y", "zh", "zl")
MP = ("x", "c")

hash_factor = 73244475
sign_factor = ((hash_factor + (1 << 16)) << 15) % (1 << 32)
sign_factor = sign_factor - (1 << 32) if sign_factor >= (1 << 31) else sign_factor


def swap(parts, axes):
    return lax.all_to_all(parts, axes, split_axis=0, concat_axis=0, tiled=True)


def from_everyone(value, axes):
    return swap(jnp.broadcast_to(value, (lax.axis_size(axes), *value.shape)), axes)


def shifted(value, axes, shift):
    size = lax.axis_size(axes)
    return lax.ppermute(value, axes, [(k, (k + shift) % size) for k in range(size)])


def placed_at(parts, places):
    out = jnp.zeros((len(parts), *parts[0].shape), parts[0].dtype)
    for part, place in zip(parts, places, strict=True):
        out = lax.dynamic_update_slice_in_dim(out, part[None], place, 0)
    return out


def part_of(parts, place):
    return lax.dynamic_index_in_dim(parts, place, 0, keepdims=False)


def sketch_kernel(where, *refs):
    pieces, out, total = refs[:-2], refs[-2], refs[-1]
    seed, first, start = where[0], where[1], where[2]
    depth, width = 2, pieces[0].shape[2]
    cols = out.shape[1]
    shape = (depth * width, 128)
    row = lax.broadcasted_iota(jnp.int32, shape, 0)
    coord = (row // width) * VW + row % width + first
    column = lax.broadcasted_iota(jnp.int32, (1, cols), 1) + start
    low = (column ^ (seed & (K - 1))) * hash_factor
    seed_high = lax.shift_right_logical(seed, 13)

    total[...] = jnp.zeros_like(total)

    def step(k, carry):
        high = (((coord + k * (depth * VW)) ^ seed_high) << 13) * hash_factor
        grads = jnp.concatenate(
            [jnp.concatenate([p[k * depth + d] for p in pieces], axis=0) for d in range(depth)],
            axis=1,
        )
        for t in range(0, cols, 256):
            tiles = []
            for u in range(t, t + 256, 128):
                mixed = high + low[:, u : u + 128]
                mixed = mixed ^ lax.shift_right_logical(mixed, 16)
                mixed = mixed * sign_factor
                tiles.append(jnp.where(mixed < 0, -1.0, 1.0).astype(jnp.bfloat16))
            signs = jnp.concatenate(tiles, axis=1)
            total[:, t : t + 256] += jnp.dot(grads, signs, preferred_element_type=jnp.float32)
        return carry

    lax.fori_loop(0, R // depth, step, 0, unroll=True)
    out[...] = total[...].astype(out.dtype)


def sketched(where, pieces, cols, dtype):
    rows = sum(p.shape[1] for p in pieces)
    flops = 2 * rows * cols * pieces[0].shape[0] * pieces[0].shape[2]
    return pl.pallas_call(
        sketch_kernel,
        out_shape=jax.ShapeDtypeStruct((rows, cols), dtype),
        in_specs=[pl.BlockSpec(memory_space=pltpu.SMEM)]
        + [pl.BlockSpec(memory_space=pltpu.VMEM)] * len(pieces),
        out_specs=pl.BlockSpec(memory_space=pltpu.VMEM),
        scratch_shapes=[pltpu.VMEM((rows, cols), jnp.float32)],
        cost_estimate=pl.CostEstimate(
            flops=flops, bytes_accessed=rows * cols * 4, transcendentals=0
        ),
        compiler_params=pltpu.CompilerParams(vmem_limit_bytes=24 << 20),
        name="sketch",
    )(where, *pieces)


def local_grads(inputs, out_grads):
    return jnp.einsum("ntr,ntj->nrj", inputs, out_grads, preferred_element_type=jnp.float32).astype(
        jnp.bfloat16
    )


def shards(train_in, train_out_grad, query_in, query_out_grad, query_owner, sketch_seed):
    examples, _, width = train_out_grad.shape
    queries = query_in.shape[0]
    ny, nzh, nzl, nx, nc = (lax.axis_size(a) for a in ("y", "zh", "zl", "x", "c"))
    nz = nzh * nzl
    coords_here = R * width

    train_grads = local_grads(train_in, train_out_grad)
    x, y, c, _, zl = (lax.axis_index(a) for a in ("x", "y", "c", "zh", "zl"))
    by_rank = train_grads.swapaxes(0, 1)
    pieces = [by_rank] + [shifted(by_rank, "y", -k) for k in range(1, ny)]

    query_grads = local_grads(query_in, query_out_grad)
    owners = query_owner[:, 0]
    later = lax.broadcasted_iota(jnp.int32, (queries, queries), 0)
    earlier = (owners[:, None] == owners[None, :]) & (
        lax.broadcasted_iota(jnp.int32, (queries, queries), 1) < later
    )
    slot = jnp.sum(earlier.astype(jnp.int32), axis=1)
    capacity = 2
    target = owners * capacity + slot
    placing = (
        lax.broadcasted_iota(jnp.int32, (ny * nz * capacity, queries), 0) == target[None, :]
    ).astype(jnp.bfloat16)
    outgoing = jnp.dot(
        placing, query_grads.reshape(queries, coords_here), preferred_element_type=jnp.float32
    ).astype(jnp.bfloat16)
    arrived = swap(outgoing.reshape(ny * nz, capacity, coords_here), DP)

    half_cols = K // ny // nc
    first = lax.axis_index(MP) * width
    halves = []
    for half, dtype in ((1 - c, jnp.bfloat16), (c, jnp.float32)):
        start = (y * nc + half) * half_cols
        where = jnp.stack([sketch_seed[0], first, start])
        halves.append(sketched(where, pieces, half_cols, dtype))
    traded = shifted(halves[0], "c", 1)
    kept, traded = (h.reshape(ny, examples, half_cols) for h in (halves[1], traded))
    turn = x - y + ny
    sums = [
        part_of(kept, lax.rem(turn + k, ny)) + part_of(traded, lax.rem(turn + k, ny)).astype(jnp.float32)
        for k in range(nx)
    ]
    features = sums[0]
    sent = []
    for k in range(1, nx):
        sent.append(shifted(sums[k].astype(jnp.bfloat16), "x", k))
    for part in sent:
        features = features + part.astype(jnp.float32)
    feature_scale = 1.0 / math.sqrt(L * R * VW)
    features = (features * feature_scale).astype(jnp.bfloat16)

    near = [features] + [shifted(features, "zl", -k) for k in range(1, nzl)]
    near = placed_at(near, [lax.rem(zl + k, nzl) for k in range(nzl)])
    near = near.reshape(nzl * examples, -1)
    rows = from_everyone(features, "zh").reshape(nc, (nzh // nc) * examples, -1)
    cols = [near]
    for k in range(1, nx):
        cols.append(shifted(near, "x", -k))
    cols = jnp.stack(cols)
    kept, given = (
        jnp.einsum("tmk,nk->tmn", cols, part_of(rows, h), preferred_element_type=jnp.float32)
        for h in (c, 1 - c)
    )
    traded = shifted(given.astype(jnp.bfloat16), "c", 1)
    gram = lax.optimization_barrier(kept) + traded.astype(jnp.float32)
    gram = jnp.stack([part_of(gram, lax.rem(k - x + nx, nx)) for k in range(ny)])
    gram = gram.astype(jnp.bfloat16).reshape(ny * nzl, examples, -1)
    gram = swap(gram, ("y", "zl"))
    gram = gram.reshape(ny, nzl, examples, -1).astype(jnp.float32).sum(axis=0)
    gram = gram * (1.0 / math.sqrt(K))
    gram = gram.reshape(nzl, examples, nzh // nc, examples).transpose(2, 0, 3, 1)
    gram = gram.reshape(-1, examples)

    scores = jnp.einsum(
        "ic,nc->in",
        arrived.reshape(ny * nz * capacity, coords_here),
        train_grads.reshape(examples, coords_here),
        preferred_element_type=jnp.float32,
    )
    score_scale = 1.0 / (L * math.sqrt(R * VW))
    scores = scores.reshape(-1, 2 * examples)
    for axis, size, bit in (("c", nc, 1), ("x", nx, 1), ("x", nx, 2)):
        scores = scores + lax.ppermute(scores, axis, [(k, k ^ bit) for k in range(size)])
    scores = scores * score_scale
    return gram, scores.reshape(1, ny * nz, capacity, examples)


def solution(mesh):
    finer = Mesh(mesh.devices.reshape(4, 4, 4, 4, 2), ("y", "zh", "zl", "x", "c"))
    placed = (
        P(DP, None, None),
        P(DP, None, MP),
        P(DP, None, None),
        P(DP, None, MP),
        P(DP, None),
        P(),
    )
    return jax.shard_map(
        shards,
        mesh=finer,
        in_specs=placed,
        out_specs=(P(MP, DP), P(DP, None, None, None)),
        check_vma=False,
    )
```
